32 devices in a mesh: mem: 4 (over z), gx: 4 (over y, core), gy: 2 (over x).
Axes of the slice: x: 2, y: 2, z: 4, core: 2. Of those that a mesh axis runs over, the one named last changes fastest.
Arguments:
- height: float32 [4, 4, 128, 256], P('mem', None, 'gx', 'gy'), may hold values from -4 to 4
- wind: float32 [4, 2, 4, 128, 256], P('mem', None, None, 'gx', 'gy'), may hold values from -0.8 to 0.8
- moisture: float32 [4, 4, 128, 256], P('mem', None, 'gx', 'gy'), may hold values from 0 to 2
- coeffs: float32 [4, 4, 4, 16384], P('mem', None, None, ('gx', 'gy')), may hold values from -6 to 6
- damping: float32 [16384], P(('gx', 'gy')), may hold values from 0.3 to 1
- vmix: float32 [4, 4], replicated, may hold values from -3 to 3
- basis: bfloat16 [16384, 384], P(('gx', 'gy')), may hold values from -0.046875 to 0.046875
- edge_source: int32 [768], replicated, may hold values from 0 to 383
- row_cell: int32 [128], replicated, may hold values from 0 to 15, never falling along the last dimension, each value on 1 to 16 neighbouring positions
- col_cell: int32 [256], replicated, may hold values from 0 to 31, never falling along the last dimension, each value on 1 to 16 neighbouring positions
- cond_rate: float32 [4], replicated, may hold values from 0.05 to 0.5
- saturation: float32 [4], replicated, may hold values from 0.5 to 1.5
- ancestry: int32 [4], replicated, may hold values from 0 to 3
Outputs:
- height_out: float32 [4, 4, 128, 256], P('mem', None, 'gx', 'gy')
- wind_out: float32 [4, 2, 4, 128, 256], P('mem', None, None, 'gx', 'gy')
- moisture_out: float32 [4, 4, 128, 256], P('mem', None, 'gx', 'gy')
- rainfall: float32 [4, 128, 256], P('mem', 'gx', 'gy')
- restricted: float32 [4, 4, 16, 32], P('mem')
- coeffs_out: float32 [4, 4, 4, 16384], P('mem', None, None, ('gx', 'gy'))
The draws below stay inside these ranges and needn't reach their ends.
Inputs may be any that keep to these rules, and one draw needn't show every extreme that they name: row_cell never falls, and each of the 16 global rows holds 1 to 16 nest rows, one exactly 16. col_cell never falls, and each of the 32 global columns holds 1 to 16 nest columns, one exactly 16.
All inputs are finite; a program needn't handle non-finite values.
Results may differ from the reference program's by a relative error of at most 0.00035.
Values sent between devices are 32-bit elements; how exact they have to be, the bound alone decides.
A program may use at most 64 MiB of HBM per device.

```python
import math
import jax
import jax.numpy as jnp
import numpy as np
from jax import lax

LEV = 4
RATIO = 8
RIM_G = 384
NSTEP = 1
ACOUSTIC = 2
MEMBERS = 4
NX = 128
NY = 256
KSPEC = 16384
GRX = 16
GRY = 32


def plant(entries, own_key, smallest, top_value):
    longest = entries.shape.index(max(entries.shape))
    spots = []
    for shift in (0, 1):
        where = [jax.random.randint(jax.random.fold_in(own_key, axis), (), 0, length) for axis, length in enumerate(entries.shape)]
        where[longest] = (where[longest] + shift) % entries.shape[longest]
        spots.append(tuple(where))
    return entries.at[spots[0]].set(smallest).at[spots[1]].set(top_value)


def shard_levels(own_key, extent, cuts, smallest, largest):
    level, own = 1.0, jax.random.fold_in(own_key, 6)
    for axis_at, shards_of in cuts:
        draws = jnp.exp(jax.random.uniform(jax.random.fold_in(own, axis_at), (shards_of,), jnp.float32, smallest / len(cuts), largest / len(cuts)))
        level = level * jnp.repeat(draws, extent[axis_at] // shards_of).reshape([-1 if axis == axis_at else 1 for axis in range(len(extent))])
    return level


def length_profile(number_of, total, most, skew):
    weights = [(1 << 20) // math.isqrt(rank ** skew) + 1 for rank in range(2, number_of + 1)]
    surplus, counts = total - most - (number_of - 1), [1] * (number_of - 1)
    while surplus > 0:
        movable = [i for i in range(number_of - 1) if counts[i] < most]
        pool, remaining = sum([weights[i] for i in movable]), surplus
        for i in movable:
            extra = min(most - counts[i], max(1, remaining * weights[i] // pool), surplus)
            counts[i] = counts[i] + extra
            surplus = surplus - extra
    return np.array([most] + counts)


def uneven_parts(stream_key, number_of, total, most, slope):
    if number_of == 2:
        one = jax.random.randint(stream_key, (), max(1, total - most), min(most, total - 1) + 1)
        return jnp.stack([one, total - one])
    tallies = jnp.asarray(length_profile(number_of, total, most, slope), jnp.int32)
    twos = (number_of - 1) // 2
    donor, receiver = tallies[1:1 + 2 * twos:2], tallies[2:2 + 2 * twos:2]
    room = jnp.minimum(donor - 1, most - receiver)
    shifted = jax.random.randint(jax.random.fold_in(stream_key, 1), (twos,), 0, 1 << 20) % (room + 1)
    tallies = tallies.at[1:1 + 2 * twos:2].set(donor - shifted).at[2:2 + 2 * twos:2].set(receiver + shifted)
    return tallies[jax.random.permutation(jax.random.fold_in(stream_key, 2), number_of)]


def centred(own_key, dims, scale, limit, shards=(), kind=jnp.bfloat16):
    entries = jax.random.normal(own_key, dims, jnp.float32) * scale
    if len(shards) > 0:
        entries = shard_levels(own_key, dims, shards, -0.22, 0.18) * entries
    return jnp.clip(entries, min=-limit, max=limit).astype(kind)


def setup_inputs(seed: int = 0) -> dict:
    key_of = jax.random.split(jax.random.key(seed), 14)
    height = centred(key_of[0], (MEMBERS, LEV, NX, NY), 1.0, 4.0, ((0, 4), (2, 4), (3, 2)), jnp.float32)
    wind = jnp.clip(jax.random.uniform(key_of[1], (MEMBERS, 2, LEV, NX, NY), jnp.float32, -0.8, 0.8) * shard_levels(key_of[1], (MEMBERS, 2, LEV, NX, NY), ((0, 4), (3, 4), (4, 2)), -0.4, 0.0), -0.8, 0.8)
    moisture = jnp.clip(2.0 * jax.random.uniform(key_of[2], (MEMBERS, LEV, NX, NY), jnp.float32) ** shard_levels(key_of[2], (MEMBERS, LEV, NX, NY), ((0, 4), (2, 4), (3, 2)), -0.2, 0.2), 0.0, 2.0)
    coeffs = centred(key_of[3], (MEMBERS, 4, LEV, KSPEC), 1.0, 6.0, ((0, 4), (3, 8)), jnp.float32)
    damping = jnp.clip(jnp.exp(math.log(1.0) - 1.2039728 * jax.random.uniform(key_of[4], (KSPEC,), jnp.float32) ** shard_levels(key_of[4], (KSPEC,), ((0, 8),), -0.2, 0.2)), 0.3, 1.0)
    vmix = centred(key_of[5], (LEV, LEV), LEV ** -0.5, 3.0, (), jnp.float32)
    basis = centred(key_of[6], (KSPEC, RIM_G), KSPEC ** -0.5, 0.046875, ((0, 8),))
    edge_source = plant(jax.random.randint(key_of[7], (2 * NX + 2 * NY,), 0, RIM_G), jax.random.fold_in(key_of[7], 1), 0, RIM_G - 1).astype(jnp.int32)
    row_cell = jnp.searchsorted(jnp.cumsum(uneven_parts(key_of[8], GRX, NX, 2 * RATIO, 0)), jnp.arange(NX), side="right").astype(jnp.int32)
    col_cell = jnp.searchsorted(jnp.cumsum(uneven_parts(key_of[9], GRY, NY, 2 * RATIO, 0)), jnp.arange(NY), side="right").astype(jnp.int32)
    cond_rate = jnp.clip(jnp.exp(jax.random.uniform(key_of[10], (LEV,), jnp.float32, math.log(0.05), math.log(0.5))), 0.05, 0.5)
    saturation = jnp.clip(jax.random.uniform(key_of[11], (LEV,), jnp.float32, 0.5, 1.5), 0.5, 1.5)
    ancestry = plant(jax.random.randint(key_of[12], (MEMBERS,), 0, MEMBERS), jax.random.fold_in(key_of[12], 1), 0, MEMBERS - 1).astype(jnp.int32)
    return dict(height=height, wind=wind, moisture=moisture, coeffs=coeffs, damping=damping, vmix=vmix, basis=basis, edge_source=edge_source, row_cell=row_cell, col_cell=col_cell, cond_rate=cond_rate, saturation=saturation, ancestry=ancestry)


acoustic_substep = 0.2
drift_step = 0.4


def framed_field(field, western_edge, eastern_edge, southern_edge, northern_edge):
    padded = jnp.pad(field, ((0, 0), (1, 1), (1, 1)))
    padded = padded.at[:, 0, 1:-1].set(western_edge)
    padded = padded.at[:, -1, 1:-1].set(eastern_edge)
    padded = padded.at[:, 1:-1, 0].set(southern_edge)
    padded = padded.at[:, 1:-1, -1].set(northern_edge)
    return padded


def member_run(height, uwind, meridional_wind, moist, western_edge, eastern_edge, southern_edge, northern_edge, cond_rate, saturation):
    rain = jnp.zeros(height.shape[1:], jnp.float32)
    for step in range(NSTEP):
        for substep in range(ACOUSTIC):
            hpad = framed_field(height, western_edge[0], eastern_edge[0], southern_edge[0], northern_edge[0])
            uwind = uwind - acoustic_substep * (hpad[:, 2:, 1:-1] - hpad[:, :-2, 1:-1])
            meridional_wind = meridional_wind - acoustic_substep * (hpad[:, 1:-1, 2:] - hpad[:, 1:-1, :-2])
            zonal_wind_padded = framed_field(uwind, western_edge[1], eastern_edge[1], southern_edge[1], northern_edge[1])
            meridional_wind_padded = framed_field(meridional_wind, western_edge[2], eastern_edge[2], southern_edge[2], northern_edge[2])
            height = height - acoustic_substep * ((zonal_wind_padded[:, 2:, 1:-1] - zonal_wind_padded[:, :-2, 1:-1]) + (meridional_wind_padded[:, 1:-1, 2:] - meridional_wind_padded[:, 1:-1, :-2]))
        qpad = framed_field(moist, western_edge[3], eastern_edge[3], southern_edge[3], northern_edge[3])
        flux = (jnp.maximum(uwind, 0.0) * (moist - qpad[:, :-2, 1:-1]) + jnp.minimum(uwind, 0.0) * (qpad[:, 2:, 1:-1] - moist)) + (jnp.maximum(meridional_wind, 0.0) * (moist - qpad[:, 1:-1, :-2]) + jnp.minimum(meridional_wind, 0.0) * (qpad[:, 1:-1, 2:] - moist))
        moist = moist - drift_step * flux
        excess = jnp.maximum(moist - saturation[:, None, None], 0.0)
        fallen = cond_rate[:, None, None] * excess
        moist = moist - fallen
        rain = rain + jnp.sum(fallen, axis=0)
    return height, uwind, meridional_wind, moist, rain


def reference(height, wind, moisture, coeffs, damping, vmix, basis, edge_source, row_cell, col_cell, cond_rate, saturation, ancestry):
    coeff_new = jnp.einsum('lj,mfjk->mflk', vmix, coeffs, precision=lax.Precision.HIGHEST) * damping
    coeff_low = coeff_new.astype(jnp.bfloat16).reshape(MEMBERS * 4 * LEV, KSPEC)
    rim = jnp.dot(coeff_low, basis, preferred_element_type=jnp.float32).reshape(MEMBERS, 4, LEV, RIM_G)
    west_all = jnp.take(rim, edge_source[:NY], axis=3)
    east_all = jnp.take(rim, edge_source[NY:2 * NY], axis=3)
    south_all = jnp.take(rim, edge_source[2 * NY:2 * NY + NX], axis=3)
    north_all = jnp.take(rim, edge_source[2 * NY + NX:], axis=3)
    row_table = (row_cell[None, :] == jnp.arange(GRX, dtype=jnp.int32)[:, None]).astype(jnp.float32)
    col_table = (col_cell[None, :] == jnp.arange(GRY, dtype=jnp.int32)[:, None]).astype(jnp.float32)
    row_count = jnp.sum(row_table, axis=1)
    col_count = jnp.sum(col_table, axis=1)
    heights, winds, moists, rains, coarses = [], [], [], [], []
    for member in range(MEMBERS):
        h_new, u_new, v_new, q_new, rain = member_run(height[member], wind[member, 0], wind[member, 1], moisture[member], west_all[member], east_all[member], south_all[member], north_all[member], cond_rate, saturation)
        partial_value = jnp.einsum('ax,lxy->lay', row_table, q_new, precision=lax.Precision.HIGHEST)
        sums = jnp.einsum('lay,by->lab', partial_value, col_table, precision=lax.Precision.HIGHEST)
        coarses.append(sums / (row_count[:, None] * col_count[None, :]))
        heights.append(h_new)
        winds.append(jnp.stack([u_new, v_new]))
        moists.append(q_new)
        rains.append(rain)
    height_all = jnp.stack(heights)
    wind_all = jnp.stack(winds)
    moist_all = jnp.stack(moists)
    rain_all = jnp.stack(rains)
    coarse_all = jnp.stack(coarses)
    return (jnp.take(height_all, ancestry, axis=0), jnp.take(wind_all, ancestry, axis=0), jnp.take(moist_all, ancestry, axis=0), jnp.take(rain_all, ancestry, axis=0), jnp.take(coarse_all, ancestry, axis=0), jnp.take(coeff_new, ancestry, axis=0))
```

```python
import functools

import jax
import jax.numpy as jnp
from jax import lax
from jax.experimental import pallas as pl
from jax.experimental.pallas import tpu as pltpu
from jax.sharding import PartitionSpec as P

RATIO = 8
ACOUSTIC = 2
HALO = 8

acoustic_substep = 0.2
drift_step = 0.4

MESH = pl.DeviceIdType.MESH


def kernel(
    sizes,
    height,
    wind,
    moisture,
    coeffs,
    damping,
    vmix,
    basis,
    edge_source,
    row_cell,
    col_cell,
    cond_rate,
    saturation,
    ancestry,
    height_out,
    wind_out,
    moisture_out,
    rain_out,
    coarse_out,
    coeffs_out,
    basis_buf,
    spec_a,
    spec_b,
    state_0,
    state_1,
    state_2,
    state_3,
    coarse_all,
    relay_spec,
    relay_state,
    relay_coarse,
    packed,
    packed_in,
    diag_in,
    rows_h,
    rows_w,
    rows_q,
    rim_part,
    rim_in,
    rim_full,
    table,
    sides,
    sides_t,
    coarse_rows_buf,
    coarse_part,
    coarse_in,
    basis_sem,
    halo_send,
    halo_recv,
    rim_send,
    rim_recv,
    rimg_send,
    rimg_recv,
    crs_send,
    crs_recv,
    mem_send,
    mem_recv,
):
    members, count_x, count_y = sizes
    plane = count_x * count_y
    levels = height.shape[1]
    size_x = height.shape[2]
    size_y = height.shape[3]
    full_x = row_cell.shape[1]
    full_y = col_cell.shape[1]
    rim_points = basis.shape[1]
    coarse_x = coarse_out.shape[2]
    coarse_y = coarse_out.shape[3]
    share = rim_part.shape[1]
    f32 = jnp.float32

    z = lax.axis_index("mem")
    ix = lax.axis_index("gx")
    iy = lax.axis_index("gy")
    here = ix * count_y + iy
    inner = jnp.logical_and(z > 0, z < members - 1)
    outer = jnp.logical_not(inner)
    across = jnp.where(z < 2, 2, 1)
    near = jnp.where(z < 2, 1, 2)
    outward = jnp.where(z < 2, 0, 3)

    fetch = pltpu.make_async_copy(basis, basis_buf, basis_sem)
    fetch.start()

    def plane_peer(step):
        other = lax.rem(here + step, plane)
        return other, other // count_y, lax.rem(other, count_y)

    barrier = pltpu.get_barrier_semaphore()
    for step in range(1, plane):
        _, px, py = plane_peer(step)
        pl.semaphore_signal(barrier, inc=1, device_id=(z, px, py), device_id_type=MESH)
    for step in range(1, members):
        pl.semaphore_signal(
            barrier,
            inc=1,
            device_id=(lax.rem(z + step, members), ix, iy),
            device_id_type=MESH,
        )

    new_fields = []
    for f in range(4):
        c = coeffs[0, f]
        acc = vmix[:, 0:1] * c[0:1]
        for j in range(1, levels):
            acc = acc + vmix[:, j : j + 1] * c[j : j + 1]
        new_fields.append(acc * damping[...])
    for f in range(4):
        buf = spec_a if f < 2 else spec_b
        buf[z, f % 2] = new_fields[f]

    lane = lax.broadcasted_iota(jnp.int32, (size_x, size_y), 1)
    fields = [height[0, l] for l in range(levels)]
    fields += [wind[0, 0, l] for l in range(levels)]
    fields += [wind[0, 1, l] for l in range(levels)]
    fields += [moisture[0, l] for l in range(levels)]
    width = size_y // (4 * levels)
    half = width // 2
    pack = jnp.zeros((size_x, size_y), f32)
    for k in range(4 * levels):
        moved = pltpu.roll(fields[k], (width * k + half) % size_y, 1)
        pack = jnp.where(lane // width == k, moved, pack)
    packed[...] = pack

    pl.semaphore_wait(barrier, plane - 1 + members - 1)

    chunks = [spec_a, spec_b, state_0, state_1, state_2, state_3, coarse_all]
    relays = [relay_spec.at[0], relay_spec.at[1]]
    relays += [relay_state.at[l] for l in range(levels)] + [relay_coarse]

    def to_across(c):
        return pltpu.make_async_remote_copy(
            src_ref=chunks[c].at[z],
            dst_ref=chunks[c].at[z],
            send_sem=mem_send.at[c, 0],
            recv_sem=mem_recv.at[c, z],
            device_id=(across, ix, iy),
            device_id_type=MESH,
        )

    def to_near(c):
        return pltpu.make_async_remote_copy(
            src_ref=chunks[c].at[z],
            dst_ref=chunks[c].at[z],
            send_sem=mem_send.at[c, 1],
            recv_sem=mem_recv.at[c, z],
            device_id=(near, ix, iy),
            device_id_type=MESH,
        )

    def to_outward(c):
        return pltpu.make_async_remote_copy(
            src_ref=relays[c],
            dst_ref=chunks[c].at[z],
            send_sem=mem_send.at[c, 1],
            recv_sem=mem_recv.at[c, z],
            device_id=(outward, ix, iy),
            device_id_type=MESH,
        )

    def arrival(c, source):
        return pltpu.make_async_remote_copy(
            src_ref=chunks[c].at[source],
            dst_ref=chunks[c].at[source],
            send_sem=mem_send.at[c, 0],
            recv_sem=mem_recv.at[c, source],
            device_id=(across, ix, iy),
            device_id_type=MESH,
        )

    def send_own(c):
        to_across(c).start()

        @pl.when(outer)
        def _():
            to_near(c).start()

    send_own(0)

    def halo_jobs(start):
        for dx in (-1, 0, 1):
            for dy in (-1, 0, 1):
                if dx == 0 and dy == 0:
                    continue
                ok = jnp.bool_(True)
                if dx == -1:
                    ok = jnp.logical_and(ok, ix > 0)
                if dx == 1:
                    ok = jnp.logical_and(ok, ix < count_x - 1)
                if dy == -1:
                    ok = jnp.logical_and(ok, iy > 0)
                if dy == 1:
                    ok = jnp.logical_and(ok, iy < count_y - 1)
                sx = 0 if dx == -1 else 1
                sy = 0 if dy == -1 else 1
                rows = pl.ds(0, HALO) if dx == -1 else pl.ds(size_x - HALO, HALO)
                target = (z, ix + dx, iy + dy)

                def go(dx=dx, dy=dy, sx=sx, sy=sy, rows=rows, target=target):
                    if dy == 0:
                        pairs = [
                            (height.at[0, :, rows, :], rows_h.at[sx]),
                            (wind.at[0, :, :, rows, :], rows_w.at[sx]),
                            (moisture.at[0, :, rows, :], rows_q.at[sx]),
                        ]
                        base = 3 * sx
                    elif dx == 0:
                        pairs = [(packed, packed_in.at[sy])]
                        base = 6 + sy
                    else:
                        pairs = [(packed.at[rows, :], diag_in.at[sx, sy])]
                        base = 8 + 2 * sx + sy
                    for n, (src, dst) in enumerate(pairs):
                        copy = pltpu.make_async_remote_copy(
                            src_ref=src,
                            dst_ref=dst,
                            send_sem=halo_send.at[base + n],
                            recv_sem=halo_recv.at[base + n],
                            device_id=target,
                            device_id_type=MESH,
                        )
                        if start == "start":
                            copy.start()
                        elif start == "send":
                            copy.wait_send()
                        else:
                            copy.wait_recv()

                if start == "recv":
                    ok = jnp.bool_(True)
                    if dx == -1:
                        ok = jnp.logical_and(ok, ix < count_x - 1)
                    if dx == 1:
                        ok = jnp.logical_and(ok, ix > 0)
                    if dy == -1:
                        ok = jnp.logical_and(ok, iy < count_y - 1)
                    if dy == 1:
                        ok = jnp.logical_and(ok, iy > 0)
                pl.when(ok)(go)

    halo_jobs("start")

    low = jnp.concatenate(new_fields, axis=0).astype(jnp.bfloat16)
    fetch.wait()
    part = jnp.dot(low, basis_buf[...], preferred_element_type=f32)
    for g in range(count_x):
        rim_part[g] = part[g * share : (g + 1) * share]

    def rim_copy(step):
        _, px, py = plane_peer(step)
        return pltpu.make_async_remote_copy(
            src_ref=rim_part.at[px],
            dst_ref=rim_in.at[here],
            send_sem=rim_send.at[step],
            recv_sem=rim_recv.at[here],
            device_id=(z, px, py),
            device_id_type=MESH,
        )

    for step in range(1, plane):
        rim_copy(step).start()
    send_own(1)

    n_edge = edge_source.shape[1]
    table[...] = (
        (lax.broadcasted_iota(jnp.int32, (rim_points, n_edge), 0) == edge_source[...])
        .astype(f32)
        .astype(jnp.bfloat16)
    )
    row_table = (
        lax.broadcasted_iota(jnp.int32, (coarse_x, full_x), 0) == row_cell[...]
    ).astype(f32)
    row_count = jnp.sum(row_table, axis=1, keepdims=True)
    wide = lax.rem(
        lax.broadcasted_iota(jnp.int32, (levels * coarse_y, full_y), 0), coarse_y
    )
    col_table = (wide == col_cell[...]).astype(f32)
    col_count = lax.dot_general(
        jnp.ones((8, full_y), f32),
        col_table,
        (((1,), (1,)), ((), ())),
        preferred_element_type=f32,
    )[0:1]
    col_off = pl.multiple_of(iy * size_y, 128)
    row_off = pl.multiple_of(ix * size_x, 8)
    cells_here = col_cell[:, pl.ds(col_off, size_y)]
    wide_here = lax.broadcasted_iota(jnp.int32, (levels * coarse_y, size_y), 0)
    coarse_rows_buf[...] = jnp.zeros_like(coarse_rows_buf)

    total = rim_part[ix]
    for step in range(1, plane):
        other, px, py = plane_peer(step)
        pltpu.make_async_remote_copy(
            src_ref=rim_part.at[px],
            dst_ref=rim_in.at[other],
            send_sem=rim_send.at[step],
            recv_sem=rim_recv.at[other],
            device_id=(z, px, py),
            device_id_type=MESH,
        ).wait_recv()
        total = total + rim_in[other]
    rim_full[ix] = total

    def rimg_copy(step, source):
        return pltpu.make_async_remote_copy(
            src_ref=rim_full.at[source],
            dst_ref=rim_full.at[source],
            send_sem=rimg_send.at[step],
            recv_sem=rimg_recv.at[source],
            device_id=(z, lax.rem(ix + step, count_x), iy),
            device_id_type=MESH,
        )

    for step in range(1, count_x):
        rimg_copy(step, ix).start()

    halo_jobs("recv")
    lane2 = lax.broadcasted_iota(jnp.int32, (size_x + 2 * HALO, size_y), 1)
    take_next = lax.rem(lane2, width) >= half
    nxt = jnp.concatenate([packed_in[0], diag_in[0, 0], diag_in[1, 0]], axis=0)
    prv = jnp.concatenate([packed_in[1], diag_in[0, 1], diag_in[1, 1]], axis=0)
    mixed = jnp.where(take_next, nxt, prv)

    ext_x = size_x + 2 * HALO
    ext_y = 2 * size_y
    rpos = lax.broadcasted_iota(jnp.int32, (ext_x, ext_y), 0)
    cpos = lax.broadcasted_iota(jnp.int32, (ext_x, ext_y), 1)
    gx_pos = ix * size_x + jnp.where(rpos < size_x + HALO, rpos, rpos - ext_x)
    gy_pos = iy * size_y + jnp.where(cpos < size_y + size_y // 2, cpos, cpos - ext_y)
    inside = (gx_pos >= 0) & (gx_pos < full_x) & (gy_pos >= 0) & (gy_pos < full_y)
    at_west = gx_pos == -1
    at_east = gx_pos == full_x
    at_south = gy_pos == -1

    for step in range(1, count_x):
        rimg_copy(step, lax.rem(ix + step, count_x)).wait_recv()
    rim = jnp.concatenate([rim_full[g] for g in range(count_x)], axis=0)
    rim_hi = rim.astype(jnp.bfloat16)
    rim_lo = (rim - rim_hi.astype(f32)).astype(jnp.bfloat16)
    both = jnp.dot(
        jnp.concatenate([rim_hi, rim_lo], axis=0), table[...], preferred_element_type=f32
    )
    n_rows = 4 * levels
    edge = both[0:n_rows] + both[n_rows:]
    sides[...] = edge
    for s in range(2):
        first = 2 * full_y + s * full_x
        sides_t[s, HALO : HALO + full_x, :] = edge[:, first : first + full_x].T
        sides_t[s, 0:HALO, :] = jnp.zeros((HALO, n_rows), f32)
        sides_t[s, HALO + full_x :, :] = jnp.zeros((HALO, n_rows), f32)
    lane1 = lax.broadcasted_iota(jnp.int32, (n_rows, size_y), 1)

    def x_side(first):
        own = sides[:, pl.ds(pl.multiple_of(first + col_off, 128), size_y)]
        after = lax.rem(iy + 1, count_y) * size_y
        before = lax.rem(iy + count_y - 1, count_y) * size_y
        nxt_b = sides[:, pl.ds(pl.multiple_of(first + after, 128), size_y)]
        prv_b = sides[:, pl.ds(pl.multiple_of(first + before, 128), size_y)]
        return jnp.concatenate([own, jnp.where(lane1 < size_y // 2, nxt_b, prv_b)], axis=1)

    def y_side(s):
        body_rows = sides_t[s, pl.ds(pl.multiple_of(row_off + HALO, 8), size_x), :]
        above = sides_t[s, pl.ds(pl.multiple_of(row_off + HALO + size_x, 8), HALO), :]
        below = sides_t[s, pl.ds(row_off, HALO), :]
        return jnp.concatenate([body_rows, above, below], axis=0)

    west, east = x_side(0), x_side(full_y)
    south, north = y_side(0), y_side(1)

    states = [state_0, state_1, state_2, state_3]
    for l in range(levels):
        def extended(f, tile, above, below):
            k = f * levels + l
            left = jnp.concatenate([tile, above, below], axis=0)
            right = pltpu.roll(mixed, (size_y - (width * k + half)) % size_y, 1)
            return jnp.concatenate([left, right], axis=1)

        def outside(f):
            k = f * levels + l
            value = jnp.where(at_south, south[:, k : k + 1], north[:, k : k + 1])
            value = jnp.where(at_east, east[k : k + 1], value)
            return jnp.where(at_west, west[k : k + 1], value)

        def up(a):
            return pltpu.roll(a, ext_x - 1, 0)

        def down(a):
            return pltpu.roll(a, 1, 0)

        def right_of(a):
            return pltpu.roll(a, ext_y - 1, 1)

        def left_of(a):
            return pltpu.roll(a, 1, 1)

        bh, bu, bv, bq = outside(0), outside(1), outside(2), outside(3)
        h = extended(0, fields[l], rows_h[0, l], rows_h[1, l])
        u = extended(1, fields[levels + l], rows_w[0, 0, l], rows_w[1, 0, l])
        v = extended(2, fields[2 * levels + l], rows_w[0, 1, l], rows_w[1, 1, l])
        q = extended(3, fields[3 * levels + l], rows_q[0, l], rows_q[1, l])
        h = jnp.where(inside, h, bh)
        q = jnp.where(inside, q, bq)
        for substep in range(ACOUSTIC):
            u = u - acoustic_substep * (up(h) - down(h))
            v = v - acoustic_substep * (right_of(h) - left_of(h))
            u = jnp.where(inside, u, bu)
            v = jnp.where(inside, v, bv)
            h = h - acoustic_substep * ((up(u) - down(u)) + (right_of(v) - left_of(v)))
            h = jnp.where(inside, h, bh)
        flux = (
            jnp.maximum(u, 0.0) * (q - down(q)) + jnp.minimum(u, 0.0) * (up(q) - q)
        ) + (
            jnp.maximum(v, 0.0) * (q - left_of(q)) + jnp.minimum(v, 0.0) * (right_of(q) - q)
        )
        q = (q - drift_step * flux)[0:size_x, 0:size_y]
        states[l][z, 0] = h[0:size_x, 0:size_y]
        states[l][z, 1] = u[0:size_x, 0:size_y]
        states[l][z, 2] = v[0:size_x, 0:size_y]
        states[l][z, 3] = q
        send_own(2 + l)

        fallen = cond_rate[l] * jnp.maximum(q - saturation[l], 0.0)
        q_new = q - fallen
        spread = ((wide_here - l * coarse_y) == cells_here).astype(f32)
        summed = lax.dot_general(
            q_new,
            spread,
            (((1,), (1,)), ((), ())),
            precision=lax.Precision.HIGHEST,
            preferred_element_type=f32,
        )
        rows_here = pl.ds(row_off, size_x)
        coarse_rows_buf[rows_here, :] = coarse_rows_buf[rows_here, :] + summed

    coarse_part[...] = jnp.dot(
        row_table,
        coarse_rows_buf[...],
        precision=lax.Precision.HIGHEST,
        preferred_element_type=f32,
    )

    def crs_copy(step, source):
        _, px, py = plane_peer(step)
        return pltpu.make_async_remote_copy(
            src_ref=coarse_part,
            dst_ref=coarse_in.at[source],
            send_sem=crs_send.at[step],
            recv_sem=crs_recv.at[source],
            device_id=(z, px, py),
            device_id_type=MESH,
        )

    for step in range(1, plane):
        crs_copy(step, here).start()

    pick = ancestry[z]
    pick = jnp.where(z == 0, jnp.minimum(pick, 1), pick)
    pick = jnp.where(z == members - 1, jnp.maximum(pick, members - 2), pick)
    passed = jnp.where(
        z < 2, jnp.maximum(ancestry[0], 1), jnp.minimum(ancestry[members - 1], members - 2)
    )

    def pass_on(c):
        @pl.when(inner)
        def _():
            arrival(c, 0).wait_recv()
            arrival(c, members - 1).wait_recv()
            arrival(c, across).wait_recv()
            relays[c][...] = chunks[c][passed]
            to_outward(c).start()

    def settle(c):
        @pl.when(outer)
        def _():
            arrival(c, near).wait_recv()

        return chunks[c][pick]

    pass_on(0)
    pass_on(1)

    total = coarse_part[...]
    for step in range(1, plane):
        other, _, _ = plane_peer(step)
        crs_copy(step, other).wait_recv()
        total = total + coarse_in[other]
    coarse_all[z] = total / (row_count * col_count)
    send_own(6)

    for c in range(2):
        got = settle(c)
        coeffs_out[0, 2 * c] = got[0]
        coeffs_out[0, 2 * c + 1] = got[1]

    for l in range(levels):
        pass_on(2 + l)
    pass_on(6)

    rain = jnp.zeros((size_x, size_y), f32)
    for l in range(levels):
        got = settle(2 + l)
        height_out[0, l] = got[0]
        wind_out[0, 0, l] = got[1]
        wind_out[0, 1, l] = got[2]
        fallen = cond_rate[l] * jnp.maximum(got[3] - saturation[l], 0.0)
        moisture_out[0, l] = got[3] - fallen
        rain = rain + fallen
    rain_out[0] = rain
    got = settle(6)
    for l in range(levels):
        coarse_out[0, l] = got[:, l * coarse_y : (l + 1) * coarse_y]

    halo_jobs("send")
    for step in range(1, plane):
        rim_copy(step).wait_send()
        crs_copy(step, here).wait_send()
    for step in range(1, count_x):
        rimg_copy(step, ix).wait_send()
    for c in range(7):
        to_across(c).wait_send()

        @pl.when(outer)
        def _(c=c):
            to_near(c).wait_send()

        @pl.when(inner)
        def _(c=c):
            to_outward(c).wait_send()


def body(
    sizes,
    height,
    wind,
    moisture,
    coeffs,
    damping,
    vmix,
    basis,
    edge_source,
    row_cell,
    col_cell,
    cond_rate,
    saturation,
    ancestry,
):
    members, count_x, count_y = sizes
    plane = count_x * count_y
    _, levels, size_x, size_y = height.shape
    local_k = coeffs.shape[3]
    rim_points = basis.shape[1]
    full_x = row_cell.shape[0]
    full_y = col_cell.shape[0]
    n_edge = edge_source.shape[0]
    coarse_x, coarse_y = full_x // RATIO, full_y // RATIO
    share = 4 * levels // count_x
    rows = 4 * levels
    f32 = jnp.float32
    vmem = pl.BlockSpec(memory_space=pltpu.VMEM)
    smem = pl.BlockSpec(memory_space=pltpu.SMEM)
    dma = pltpu.SemaphoreType.DMA
    spec_chunk = (2, levels, local_k)
    state_chunk = (4, size_x, size_y)
    coarse_chunk = (coarse_x, levels * coarse_y)
    scratch = [
        pltpu.VMEM(basis.shape, basis.dtype),
        pltpu.VMEM((members, *spec_chunk), f32),
        pltpu.VMEM((members, *spec_chunk), f32),
        *[pltpu.VMEM((members, *state_chunk), f32) for _ in range(4)],
        pltpu.VMEM((members, *coarse_chunk), f32),
        pltpu.VMEM((2, *spec_chunk), f32),
        pltpu.VMEM((levels, *state_chunk), f32),
        pltpu.VMEM(coarse_chunk, f32),
        pltpu.VMEM((size_x, size_y), f32),
        pltpu.VMEM((2, size_x, size_y), f32),
        pltpu.VMEM((2, 2, HALO, size_y), f32),
        pltpu.VMEM((2, levels, HALO, size_y), f32),
        pltpu.VMEM((2, 2, levels, HALO, size_y), f32),
        pltpu.VMEM((2, levels, HALO, size_y), f32),
        pltpu.VMEM((count_x, share, rim_points), f32),
        pltpu.VMEM((plane, share, rim_points), f32),
        pltpu.VMEM((count_x, share, rim_points), f32),
        pltpu.VMEM((rim_points, n_edge), jnp.bfloat16),
        pltpu.VMEM((rows, n_edge), f32),
        pltpu.VMEM((2, full_x + 2 * HALO, rows), f32),
        pltpu.VMEM((full_x, levels * coarse_y), f32),
        pltpu.VMEM(coarse_chunk, f32),
        pltpu.VMEM((plane, *coarse_chunk), f32),
        dma,
        dma((12,)),
        dma((12,)),
        dma((plane,)),
        dma((plane,)),
        dma((count_x,)),
        dma((count_x,)),
        dma((plane,)),
        dma((plane,)),
        dma((7, 2)),
        dma((7, members)),
    ]
    outs = (
        jax.ShapeDtypeStruct(height.shape, f32),
        jax.ShapeDtypeStruct(wind.shape, f32),
        jax.ShapeDtypeStruct(moisture.shape, f32),
        jax.ShapeDtypeStruct((1, size_x, size_y), f32),
        jax.ShapeDtypeStruct((1, levels, coarse_x, coarse_y), f32),
        jax.ShapeDtypeStruct(coeffs.shape, f32),
    )
    return pl.pallas_call(
        functools.partial(kernel, sizes),
        out_shape=outs,
        in_specs=[
            vmem,
            vmem,
            vmem,
            vmem,
            vmem,
            vmem,
            pl.BlockSpec(memory_space=pl.ANY),
            vmem,
            vmem,
            vmem,
            smem,
            smem,
            smem,
        ],
        out_specs=(vmem,) * 6,
        scratch_shapes=scratch,
        compiler_params=pltpu.CompilerParams(
            collective_id=0, has_side_effects=True, vmem_limit_bytes=60 * 1024 * 1024
        ),
    )(
        height,
        wind,
        moisture,
        coeffs,
        damping.reshape(1, -1),
        vmix,
        basis,
        edge_source.reshape(1, -1),
        row_cell.reshape(1, -1),
        col_cell.reshape(1, -1),
        cond_rate,
        saturation,
        ancestry,
    )


def solution(mesh):
    sizes = (mesh.shape["mem"], mesh.shape["gx"], mesh.shape["gy"])
    in_specs = (
        P("mem", None, "gx", "gy"),
        P("mem", None, None, "gx", "gy"),
        P("mem", None, "gx", "gy"),
        P("mem", None, None, ("gx", "gy")),
        P(("gx", "gy")),
        P(),
        P(("gx", "gy"), None),
        P(),
        P(),
        P(),
        P(),
        P(),
        P(),
    )
    out_specs = (
        P("mem", None, "gx", "gy"),
        P("mem", None, None, "gx", "gy"),
        P("mem", None, "gx", "gy"),
        P("mem", "gx", "gy"),
        P("mem", None, None, None),
        P("mem", None, None, ("gx", "gy")),
    )
    return jax.shard_map(
        functools.partial(body, sizes),
        mesh=mesh,
        in_specs=in_specs,
        out_specs=out_specs,
        check_vma=False,
    )
```

```python
import functools

import jax
import jax.numpy as jnp
from jax import lax
from jax.experimental import pallas as pl
from jax.experimental.pallas import tpu as pltpu
from jax.sharding import PartitionSpec as P

RATIO = 8
ACOUSTIC = 2
HALO = 8

acoustic_substep = 0.2
drift_step = 0.4

MESH = pl.DeviceIdType.MESH


def kernel(
    sizes,
    height,
    wind,
    moisture,
    coeffs,
    damping,
    vmix,
    basis,
    edge_source,
    row_cell,
    col_cell,
    cond_rate,
    saturation,
    ancestry,
    height_out,
    wind_out,
    moisture_out,
    rain_out,
    coarse_out,
    coeffs_out,
    ready,
    spec_a,
    spec_b,
    state_0,
    state_1,
    state_2,
    state_3,
    coarse_all,
    relay_spec,
    relay_state,
    relay_coarse,
    packed,
    packed_in,
    diag_in,
    rows_h,
    rows_w,
    rows_q,
    rim_part,
    rim_in,
    rim_full,
    table,
    sides,
    sides_t,
    coarse_rows_buf,
    coarse_part,
    coarse_in,
    halo_send,
    halo_recv,
    rim_send,
    rim_recv,
    rimg_send,
    rimg_recv,
    crs_send,
    crs_recv,
    mem_send,
    mem_recv,
):
    members, count_x, count_y = sizes
    plane = count_x * count_y
    levels = height.shape[1]
    size_x = height.shape[2]
    size_y = height.shape[3]
    full_x = row_cell.shape[1]
    full_y = col_cell.shape[1]
    rim_points = basis.shape[1]
    coarse_x = coarse_out.shape[2]
    coarse_y = coarse_out.shape[3]
    share = rim_part.shape[1]
    f32 = jnp.float32

    z = lax.axis_index("mem")
    ix = lax.axis_index("gx")
    iy = lax.axis_index("gy")
    here = ix * count_y + iy
    inner = jnp.logical_and(z > 0, z < members - 1)
    outer = jnp.logical_not(inner)
    across = jnp.where(z < 2, 2, 1)
    near = jnp.where(z < 2, 1, 2)
    outward = jnp.where(z < 2, 0, 3)

    def plane_peer(step):
        other = lax.rem(here + step, plane)
        return other, other // count_y, lax.rem(other, count_y)

    barrier = pltpu.get_barrier_semaphore()
    for step in range(1, plane):
        _, px, py = plane_peer(step)
        pl.semaphore_signal(barrier, inc=1, device_id=(z, px, py), device_id_type=MESH)
    for step in range(1, members):
        pl.semaphore_signal(
            barrier,
            inc=1,
            device_id=(lax.rem(z + step, members), ix, iy),
            device_id_type=MESH,
        )

    ready(3, 4, 5)
    new_fields = []
    for f in range(4):
        c = coeffs[0, f]
        acc = vmix[:, 0:1] * c[0:1]
        for j in range(1, levels):
            acc = acc + vmix[:, j : j + 1] * c[j : j + 1]
        new_fields.append(acc * damping[...])
    for f in range(4):
        buf = spec_a if f < 2 else spec_b
        buf[z, f % 2] = new_fields[f]

    ready(0, 1, 2)
    lane = lax.broadcasted_iota(jnp.int32, (size_x, size_y), 1)
    fields = [height[0, l] for l in range(levels)]
    fields += [wind[0, 0, l] for l in range(levels)]
    fields += [wind[0, 1, l] for l in range(levels)]
    fields += [moisture[0, l] for l in range(levels)]
    width = size_y // (4 * levels)
    half = width // 2
    pack = jnp.zeros((size_x, size_y), f32)
    for k in range(4 * levels):
        moved = pltpu.roll(fields[k], (width * k + half) % size_y, 1)
        pack = jnp.where(lane // width == k, moved, pack)
    packed[...] = pack

    pl.semaphore_wait(barrier, plane - 1 + members - 1)

    chunks = [spec_a, spec_b, state_0, state_1, state_2, state_3, coarse_all]
    relays = [relay_spec.at[0], relay_spec.at[1]]
    relays += [relay_state.at[l] for l in range(levels)] + [relay_coarse]

    def to_across(c):
        return pltpu.make_async_remote_copy(
            src_ref=chunks[c].at[z],
            dst_ref=chunks[c].at[z],
            send_sem=mem_send.at[c, 0],
            recv_sem=mem_recv.at[c, z],
            device_id=(across, ix, iy),
            device_id_type=MESH,
        )

    def to_near(c):
        return pltpu.make_async_remote_copy(
            src_ref=chunks[c].at[z],
            dst_ref=chunks[c].at[z],
            send_sem=mem_send.at[c, 1],
            recv_sem=mem_recv.at[c, z],
            device_id=(near, ix, iy),
            device_id_type=MESH,
        )

    def to_outward(c):
        return pltpu.make_async_remote_copy(
            src_ref=relays[c],
            dst_ref=chunks[c].at[z],
            send_sem=mem_send.at[c, 1],
            recv_sem=mem_recv.at[c, z],
            device_id=(outward, ix, iy),
            device_id_type=MESH,
        )

    def arrival(c, source):
        return pltpu.make_async_remote_copy(
            src_ref=chunks[c].at[source],
            dst_ref=chunks[c].at[source],
            send_sem=mem_send.at[c, 0],
            recv_sem=mem_recv.at[c, source],
            device_id=(across, ix, iy),
            device_id_type=MESH,
        )

    def send_own(c):
        to_across(c).start()

        @pl.when(outer)
        def _():
            to_near(c).start()

    send_own(0)

    def halo_jobs(start):
        for dx in (-1, 0, 1):
            for dy in (-1, 0, 1):
                if dx == 0 and dy == 0:
                    continue
                ok = jnp.bool_(True)
                if dx == -1:
                    ok = jnp.logical_and(ok, ix > 0)
                if dx == 1:
                    ok = jnp.logical_and(ok, ix < count_x - 1)
                if dy == -1:
                    ok = jnp.logical_and(ok, iy > 0)
                if dy == 1:
                    ok = jnp.logical_and(ok, iy < count_y - 1)
                sx = 0 if dx == -1 else 1
                sy = 0 if dy == -1 else 1
                rows = pl.ds(0, HALO) if dx == -1 else pl.ds(size_x - HALO, HALO)
                target = (z, ix + dx, iy + dy)

                def go(dx=dx, dy=dy, sx=sx, sy=sy, rows=rows, target=target):
                    if dy == 0:
                        pairs = [
                            (height.at[0, :, rows, :], rows_h.at[sx]),
                            (wind.at[0, :, :, rows, :], rows_w.at[sx]),
                            (moisture.at[0, :, rows, :], rows_q.at[sx]),
                        ]
                        base = 3 * sx
                    elif dx == 0:
                        pairs = [(packed, packed_in.at[sy])]
                        base = 6 + sy
                    else:
                        pairs = [(packed.at[rows, :], diag_in.at[sx, sy])]
                        base = 8 + 2 * sx + sy
                    for n, (src, dst) in enumerate(pairs):
                        copy = pltpu.make_async_remote_copy(
                            src_ref=src,
                            dst_ref=dst,
                            send_sem=halo_send.at[base + n],
                            recv_sem=halo_recv.at[base + n],
                            device_id=target,
                            device_id_type=MESH,
                        )
                        if start == "start":
                            copy.start()
                        elif start == "send":
                            copy.wait_send()
                        else:
                            copy.wait_recv()

                if start == "recv":
                    ok = jnp.bool_(True)
                    if dx == -1:
                        ok = jnp.logical_and(ok, ix < count_x - 1)
                    if dx == 1:
                        ok = jnp.logical_and(ok, ix > 0)
                    if dy == -1:
                        ok = jnp.logical_and(ok, iy < count_y - 1)
                    if dy == 1:
                        ok = jnp.logical_and(ok, iy > 0)
                pl.when(ok)(go)

    halo_jobs("start")

    low = jnp.concatenate(new_fields, axis=0).astype(jnp.bfloat16)
    ready(6)
    part = jnp.dot(low, basis[...], preferred_element_type=f32)
    for g in range(count_x):
        rim_part[g] = part[g * share : (g + 1) * share]

    def rim_copy(step):
        _, px, py = plane_peer(step)
        return pltpu.make_async_remote_copy(
            src_ref=rim_part.at[px],
            dst_ref=rim_in.at[here],
            send_sem=rim_send.at[step],
            recv_sem=rim_recv.at[here],
            device_id=(z, px, py),
            device_id_type=MESH,
        )

    for step in range(1, plane):
        rim_copy(step).start()
    send_own(1)

    ready(7, 8, 9, 10, 11, 12)
    n_edge = edge_source.shape[0]
    table[...] = (
        (lax.broadcasted_iota(jnp.int32, (rim_points, n_edge), 0)
         == edge_source[...].reshape(1, n_edge))
        .astype(f32)
        .astype(jnp.bfloat16)
    )
    row_table = (
        lax.broadcasted_iota(jnp.int32, (coarse_x, full_x), 0) == row_cell[...]
    ).astype(f32)
    row_count = jnp.sum(row_table, axis=1, keepdims=True)
    wide = lax.rem(
        lax.broadcasted_iota(jnp.int32, (levels * coarse_y, full_y), 0), coarse_y
    )
    col_table = (wide == col_cell[...]).astype(f32)
    col_count = lax.dot_general(
        jnp.ones((8, full_y), f32),
        col_table,
        (((1,), (1,)), ((), ())),
        preferred_element_type=f32,
    )[0:1]
    col_off = pl.multiple_of(iy * size_y, 128)
    row_off = pl.multiple_of(ix * size_x, 8)
    cells_here = col_cell[:, pl.ds(col_off, size_y)]
    wide_here = lax.broadcasted_iota(jnp.int32, (levels * coarse_y, size_y), 0)
    coarse_rows_buf[...] = jnp.zeros_like(coarse_rows_buf)

    total = rim_part[ix]
    for step in range(1, plane):
        other, px, py = plane_peer(step)
        pltpu.make_async_remote_copy(
            src_ref=rim_part.at[px],
            dst_ref=rim_in.at[other],
            send_sem=rim_send.at[step],
            recv_sem=rim_recv.at[other],
            device_id=(z, px, py),
            device_id_type=MESH,
        ).wait_recv()
        total = total + rim_in[other]
    rim_full[ix] = total

    def rimg_copy(step, source):
        return pltpu.make_async_remote_copy(
            src_ref=rim_full.at[source],
            dst_ref=rim_full.at[source],
            send_sem=rimg_send.at[step],
            recv_sem=rimg_recv.at[source],
            device_id=(z, lax.rem(ix + step, count_x), iy),
            device_id_type=MESH,
        )

    for step in range(1, count_x):
        rimg_copy(step, ix).start()

    halo_jobs("recv")
    lane2 = lax.broadcasted_iota(jnp.int32, (size_x + 2 * HALO, size_y), 1)
    take_next = lax.rem(lane2, width) >= half
    nxt = jnp.concatenate([packed_in[0], diag_in[0, 0], diag_in[1, 0]], axis=0)
    prv = jnp.concatenate([packed_in[1], diag_in[0, 1], diag_in[1, 1]], axis=0)
    mixed = jnp.where(take_next, nxt, prv)

    ext_x = size_x + 2 * HALO
    ext_y = 2 * size_y
    rpos = lax.broadcasted_iota(jnp.int32, (ext_x, ext_y), 0)
    cpos = lax.broadcasted_iota(jnp.int32, (ext_x, ext_y), 1)
    gx_pos = ix * size_x + jnp.where(rpos < size_x + HALO, rpos, rpos - ext_x)
    gy_pos = iy * size_y + jnp.where(cpos < size_y + size_y // 2, cpos, cpos - ext_y)
    inside = (gx_pos >= 0) & (gx_pos < full_x) & (gy_pos >= 0) & (gy_pos < full_y)
    at_west = gx_pos == -1
    at_east = gx_pos == full_x
    at_south = gy_pos == -1

    for step in range(1, count_x):
        rimg_copy(step, lax.rem(ix + step, count_x)).wait_recv()
    rim = jnp.concatenate([rim_full[g] for g in range(count_x)], axis=0)
    rim_hi = rim.astype(jnp.bfloat16)
    rim_lo = (rim - rim_hi.astype(f32)).astype(jnp.bfloat16)
    both = jnp.dot(
        jnp.concatenate([rim_hi, rim_lo], axis=0), table[...], preferred_element_type=f32
    )
    n_rows = 4 * levels
    edge = both[0:n_rows] + both[n_rows:]
    sides[...] = edge
    for s in range(2):
        first = 2 * full_y + s * full_x
        sides_t[s, HALO : HALO + full_x, :] = edge[:, first : first + full_x].T
        sides_t[s, 0:HALO, :] = jnp.zeros((HALO, n_rows), f32)
        sides_t[s, HALO + full_x :, :] = jnp.zeros((HALO, n_rows), f32)
    lane1 = lax.broadcasted_iota(jnp.int32, (n_rows, size_y), 1)

    def x_side(first):
        own = sides[:, pl.ds(pl.multiple_of(first + col_off, 128), size_y)]
        after = lax.rem(iy + 1, count_y) * size_y
        before = lax.rem(iy + count_y - 1, count_y) * size_y
        nxt_b = sides[:, pl.ds(pl.multiple_of(first + after, 128), size_y)]
        prv_b = sides[:, pl.ds(pl.multiple_of(first + before, 128), size_y)]
        return jnp.concatenate([own, jnp.where(lane1 < size_y // 2, nxt_b, prv_b)], axis=1)

    def y_side(s):
        body_rows = sides_t[s, pl.ds(pl.multiple_of(row_off + HALO, 8), size_x), :]
        above = sides_t[s, pl.ds(pl.multiple_of(row_off + HALO + size_x, 8), HALO), :]
        below = sides_t[s, pl.ds(row_off, HALO), :]
        return jnp.concatenate([body_rows, above, below], axis=0)

    west, east = x_side(0), x_side(full_y)
    south, north = y_side(0), y_side(1)

    states = [state_0, state_1, state_2, state_3]
    for l in range(levels):
        def extended(f, tile, above, below):
            k = f * levels + l
            left = jnp.concatenate([tile, above, below], axis=0)
            right = pltpu.roll(mixed, (size_y - (width * k + half)) % size_y, 1)
            return jnp.concatenate([left, right], axis=1)

        def outside(f):
            k = f * levels + l
            value = jnp.where(at_south, south[:, k : k + 1], north[:, k : k + 1])
            value = jnp.where(at_east, east[k : k + 1], value)
            return jnp.where(at_west, west[k : k + 1], value)

        def up(a):
            return pltpu.roll(a, ext_x - 1, 0)

        def down(a):
            return pltpu.roll(a, 1, 0)

        def right_of(a):
            return pltpu.roll(a, ext_y - 1, 1)

        def left_of(a):
            return pltpu.roll(a, 1, 1)

        bh, bu, bv, bq = outside(0), outside(1), outside(2), outside(3)
        h = extended(0, fields[l], rows_h[0, l], rows_h[1, l])
        u = extended(1, fields[levels + l], rows_w[0, 0, l], rows_w[1, 0, l])
        v = extended(2, fields[2 * levels + l], rows_w[0, 1, l], rows_w[1, 1, l])
        q = extended(3, fields[3 * levels + l], rows_q[0, l], rows_q[1, l])
        h = jnp.where(inside, h, bh)
        q = jnp.where(inside, q, bq)
        for substep in range(ACOUSTIC):
            u = u - acoustic_substep * (up(h) - down(h))
            v = v - acoustic_substep * (right_of(h) - left_of(h))
            u = jnp.where(inside, u, bu)
            v = jnp.where(inside, v, bv)
            h = h - acoustic_substep * ((up(u) - down(u)) + (right_of(v) - left_of(v)))
            h = jnp.where(inside, h, bh)
        flux = (
            jnp.maximum(u, 0.0) * (q - down(q)) + jnp.minimum(u, 0.0) * (up(q) - q)
        ) + (
            jnp.maximum(v, 0.0) * (q - left_of(q)) + jnp.minimum(v, 0.0) * (right_of(q) - q)
        )
        q = (q - drift_step * flux)[0:size_x, 0:size_y]
        states[l][z, 0] = h[0:size_x, 0:size_y]
        states[l][z, 1] = u[0:size_x, 0:size_y]
        states[l][z, 2] = v[0:size_x, 0:size_y]
        states[l][z, 3] = q
        send_own(2 + l)

        fallen = cond_rate[l] * jnp.maximum(q - saturation[l], 0.0)
        q_new = q - fallen
        spread = ((wide_here - l * coarse_y) == cells_here).astype(f32)
        summed = lax.dot_general(
            q_new,
            spread,
            (((1,), (1,)), ((), ())),
            precision=lax.Precision.HIGHEST,
            preferred_element_type=f32,
        )
        rows_here = pl.ds(row_off, size_x)
        coarse_rows_buf[rows_here, :] = coarse_rows_buf[rows_here, :] + summed

    coarse_part[...] = jnp.dot(
        row_table,
        coarse_rows_buf[...],
        precision=lax.Precision.HIGHEST,
        preferred_element_type=f32,
    )

    def crs_copy(step, source):
        _, px, py = plane_peer(step)
        return pltpu.make_async_remote_copy(
            src_ref=coarse_part,
            dst_ref=coarse_in.at[source],
            send_sem=crs_send.at[step],
            recv_sem=crs_recv.at[source],
            device_id=(z, px, py),
            device_id_type=MESH,
        )

    for step in range(1, plane):
        crs_copy(step, here).start()

    pick = ancestry[z]
    pick = jnp.where(z == 0, jnp.minimum(pick, 1), pick)
    pick = jnp.where(z == members - 1, jnp.maximum(pick, members - 2), pick)
    passed = jnp.where(
        z < 2, jnp.maximum(ancestry[0], 1), jnp.minimum(ancestry[members - 1], members - 2)
    )

    def pass_on(c):
        @pl.when(inner)
        def _():
            arrival(c, 0).wait_recv()
            arrival(c, members - 1).wait_recv()
            arrival(c, across).wait_recv()
            relays[c][...] = chunks[c][passed]
            to_outward(c).start()

    def settle(c):
        @pl.when(outer)
        def _():
            arrival(c, near).wait_recv()

        return chunks[c][pick]

    pass_on(0)
    pass_on(1)

    total = coarse_part[...]
    for step in range(1, plane):
        other, _, _ = plane_peer(step)
        crs_copy(step, other).wait_recv()
        total = total + coarse_in[other]
    coarse_all[z] = total / (row_count * col_count)
    send_own(6)

    for c in range(2):
        got = settle(c)
        coeffs_out[0, 2 * c] = got[0]
        coeffs_out[0, 2 * c + 1] = got[1]

    for l in range(levels):
        pass_on(2 + l)
    pass_on(6)

    rain = jnp.zeros((size_x, size_y), f32)
    for l in range(levels):
        got = settle(2 + l)
        height_out[0, l] = got[0]
        wind_out[0, 0, l] = got[1]
        wind_out[0, 1, l] = got[2]
        fallen = cond_rate[l] * jnp.maximum(got[3] - saturation[l], 0.0)
        moisture_out[0, l] = got[3] - fallen
        rain = rain + fallen
    rain_out[0] = rain
    got = settle(6)
    for l in range(levels):
        coarse_out[0, l] = got[:, l * coarse_y : (l + 1) * coarse_y]

    halo_jobs("send")
    for step in range(1, plane):
        rim_copy(step).wait_send()
        crs_copy(step, here).wait_send()
    for step in range(1, count_x):
        rimg_copy(step, ix).wait_send()
    for c in range(7):
        to_across(c).wait_send()

        @pl.when(outer)
        def _(c=c):
            to_near(c).wait_send()

        @pl.when(inner)
        def _(c=c):
            to_outward(c).wait_send()


def staged_kernel(sizes, *refs):
    sources, outs, held = refs[:13], refs[13:19], refs[19:32]
    sems, rest = refs[-1], refs[32:-1]
    copies = [pltpu.make_async_copy(sources[n], held[n], sems.at[n]) for n in range(13)]
    for n in (3, 4, 5, 0, 1, 2, 6, 7, 8, 9, 10, 11, 12):
        copies[n].start()

    def ready(*which):
        for n in which:
            copies[n].wait()

    kernel(sizes, *held, *outs, ready, *rest)


def write_out(*refs):
    sems = refs[12]
    copies = [pltpu.make_async_copy(refs[n], refs[6 + n], sems.at[n]) for n in range(6)]
    for copy in copies:
        copy.start()
    for copy in copies:
        copy.wait()


def body(
    sizes,
    height,
    wind,
    moisture,
    coeffs,
    damping,
    vmix,
    basis,
    edge_source,
    row_cell,
    col_cell,
    cond_rate,
    saturation,
    ancestry,
):
    members, count_x, count_y = sizes
    plane = count_x * count_y
    _, levels, size_x, size_y = height.shape
    local_k = coeffs.shape[3]
    rim_points = basis.shape[1]
    full_x = row_cell.shape[0]
    full_y = col_cell.shape[0]
    n_edge = edge_source.shape[0]
    coarse_x, coarse_y = full_x // RATIO, full_y // RATIO
    share = 4 * levels // count_x
    rows = 4 * levels
    f32 = jnp.float32
    vmem = pl.BlockSpec(memory_space=pltpu.VMEM)
    dma = pltpu.SemaphoreType.DMA
    spec_chunk = (2, levels, local_k)
    state_chunk = (4, size_x, size_y)
    coarse_chunk = (coarse_x, levels * coarse_y)
    operands = (
        height,
        wind,
        moisture,
        coeffs,
        damping.reshape(1, -1),
        vmix,
        basis,
        edge_source,
        row_cell.reshape(1, -1),
        col_cell.reshape(1, -1),
        cond_rate,
        saturation,
        ancestry,
    )
    scratch = [
        *[pltpu.VMEM(a.shape, a.dtype) for a in operands[:10]],
        *[pltpu.SMEM(a.shape, a.dtype) for a in operands[10:]],
        pltpu.VMEM((members, *spec_chunk), f32),
        pltpu.VMEM((members, *spec_chunk), f32),
        *[pltpu.VMEM((members, *state_chunk), f32) for _ in range(4)],
        pltpu.VMEM((members, *coarse_chunk), f32),
        pltpu.VMEM((2, *spec_chunk), f32),
        pltpu.VMEM((levels, *state_chunk), f32),
        pltpu.VMEM(coarse_chunk, f32),
        pltpu.VMEM((size_x, size_y), f32),
        pltpu.VMEM((2, size_x, size_y), f32),
        pltpu.VMEM((2, 2, HALO, size_y), f32),
        pltpu.VMEM((2, levels, HALO, size_y), f32),
        pltpu.VMEM((2, 2, levels, HALO, size_y), f32),
        pltpu.VMEM((2, levels, HALO, size_y), f32),
        pltpu.VMEM((count_x, share, rim_points), f32),
        pltpu.VMEM((plane, share, rim_points), f32),
        pltpu.VMEM((count_x, share, rim_points), f32),
        pltpu.VMEM((rim_points, n_edge), jnp.bfloat16),
        pltpu.VMEM((rows, n_edge), f32),
        pltpu.VMEM((2, full_x + 2 * HALO, rows), f32),
        pltpu.VMEM((full_x, levels * coarse_y), f32),
        pltpu.VMEM(coarse_chunk, f32),
        pltpu.VMEM((plane, *coarse_chunk), f32),
        dma((12,)),
        dma((12,)),
        dma((plane,)),
        dma((plane,)),
        dma((count_x,)),
        dma((count_x,)),
        dma((plane,)),
        dma((plane,)),
        dma((7, 2)),
        dma((7, members)),
        dma((13,)),
    ]
    outs = (
        pltpu.VMEM(height.shape, f32),
        pltpu.VMEM(wind.shape, f32),
        pltpu.VMEM(moisture.shape, f32),
        pltpu.VMEM((1, size_x, size_y), f32),
        pltpu.VMEM((1, levels, coarse_x, coarse_y), f32),
        pltpu.VMEM(coeffs.shape, f32),
    )
    results = pl.pallas_call(
        functools.partial(staged_kernel, sizes),
        out_shape=outs,
        in_specs=[pl.BlockSpec(memory_space=pltpu.HBM)] * 13,
        out_specs=(vmem,) * 6,
        scratch_shapes=scratch,
        compiler_params=pltpu.CompilerParams(
            collective_id=0, has_side_effects=True, vmem_limit_bytes=36 * 1024 * 1024
        ),
    )(*[pltpu.with_memory_space_constraint(a, pltpu.HBM) for a in operands])
    return pl.pallas_call(
        write_out,
        out_shape=tuple(jax.ShapeDtypeStruct(r.shape, f32) for r in results),
        in_specs=[vmem] * 6,
        out_specs=(pl.BlockSpec(memory_space=pl.ANY),) * 6,
        scratch_shapes=[dma((6,))],
        compiler_params=pltpu.CompilerParams(vmem_limit_bytes=8 * 1024 * 1024),
    )(*results)


def solution(mesh):
    sizes = (mesh.shape["mem"], mesh.shape["gx"], mesh.shape["gy"])
    in_specs = (
        P("mem", None, "gx", "gy"),
        P("mem", None, None, "gx", "gy"),
        P("mem", None, "gx", "gy"),
        P("mem", None, None, ("gx", "gy")),
        P(("gx", "gy")),
        P(),
        P(("gx", "gy"), None),
        P(),
        P(),
        P(),
        P(),
        P(),
        P(),
    )
    out_specs = (
        P("mem", None, "gx", "gy"),
        P("mem", None, None, "gx", "gy"),
        P("mem", None, "gx", "gy"),
        P("mem", "gx", "gy"),
        P("mem", None, None, None),
        P("mem", None, None, ("gx", "gy")),
    )
    return jax.shard_map(
        functools.partial(body, sizes),
        mesh=mesh,
        in_specs=in_specs,
        out_specs=out_specs,
        check_vma=False,
    )
```
